256 devices in a mesh: row: 4 (over x), node: 64 (over y, z, core).
Axes of the slice: x: 4, y: 4, z: 8, core: 2. Of those that a mesh axis runs over, the one named last changes fastest.
Arguments:
- embeddings: bfloat16 [524288, 1024], P(('row', 'node'))
- row_parent: int32 [524288], P(('row', 'node')), may hold values from 0 to 511, as said below
- block_fill: int32 [256, 64], P(('row', 'node')), may hold values from 1 to 32, as said below
- child_parent: int32 [32768], P('node'), may hold values from 0 to 511, as said below
- centroids: bfloat16 [32768, 1024], P('node'), may hold values from -6 to 6
Outputs:
- new_centroids: bfloat16 [32768, 1024], P('node')
- loglik: float32 [524288], P(('row', 'node'))
The draws below stay inside these ranges and needn't reach their ends.
Inputs may be any that keep to these rules, and one draw needn't show every extreme that they name: `row_parent`: a slot in destination block j of one device's 2048 slots (slots j * 32 to (j + 1) * 32 - 1 of that device) has a parent from j * 8 to (j + 1) * 8 - 1. `block_fill`: in every draw one destination block is full (32) from every source device. `child_parent`: child k has a parent from (k // 512) * 8 to (k // 512 + 1) * 8 - 1, and every parent has at least one child.
All inputs are finite; a program needn't handle non-finite values.
Results may differ from the reference program's by a relative error of at most 0.01285.
Values may be sent and summed in bfloat16 or wider, within the bound.
A program may use at most 64 MiB of HBM per device.

```python
import jax
import jax.numpy as jnp
from jax import lax

D = 1024
KID_DEV = 512
PAR_DEV = 8
ROW_DEV = 2048
ITERS = 2
CAP = 32
ROWS = 524288
KIDS = 32768
N_ROW = 4
N_NODE = 64


def draw_embeddings(key, part):
    first = jax.random.fold_in(key, 0)
    values = jnp.clip(jax.random.normal(first, (ROWS, D), jnp.float32), -6.0, 6.0)
    return values.astype(jnp.bfloat16)


def draw_row_parent(key, part):
    index = jnp.arange(ROWS, dtype=jnp.int32)
    block = index % ROW_DEV // CAP
    offset = jax.random.randint(key, (ROWS,), 0, PAR_DEV, dtype=jnp.int32)
    offset = jnp.where(index == 0, 0, offset)
    offset = jnp.where(index == ROWS - 1, PAR_DEV - 1, offset)
    return block * PAR_DEV + offset


def draw_block_fill(key, part):
    first, second = jax.random.split(key)
    fill = jax.random.randint(first, (N_ROW * N_NODE, N_NODE), 1, CAP + 1, dtype=jnp.int32)
    column = jnp.arange(N_NODE, dtype=jnp.int32)[None, :]
    source = jnp.arange(N_ROW * N_NODE, dtype=jnp.int32)[:, None]
    full = jax.random.randint(second, (), 0, N_NODE, dtype=jnp.int32)
    fill = jnp.where(column == full, CAP, fill)
    fill = jnp.where((column == (full + 1) % N_NODE) & (source == 0), 1, fill)
    return fill


def draw_child_parent(key, part):
    index = jnp.arange(KIDS, dtype=jnp.int32)
    local = index % KID_DEV
    owner = index // KID_DEV
    extra = jax.random.randint(key, (KIDS,), 0, PAR_DEV, dtype=jnp.int32)
    return owner * PAR_DEV + jnp.where(local < PAR_DEV, local, extra)


def steps_of(rng, dims, cuts, smallest, largest):
    def one(axis_at, blocks):
        heights = jax.random.uniform(jax.random.fold_in(jax.random.fold_in(rng, 6), axis_at), (blocks,), jnp.float32, smallest / len(cuts), largest / len(cuts))
        return jnp.repeat(jnp.exp(heights), dims[axis_at] // blocks).reshape((-1,) + (1,) * (len(dims) - axis_at - 1))

    level = one(*cuts[0])
    for cut in cuts[1:]:
        level = level * one(*cut)
    return level


def noise(key, shape, width, bound, shards=(), kind=jnp.bfloat16):
    values = width * jax.random.normal(key, shape, jnp.float32)
    if shards:
        values = values * steps_of(key, shape, shards, -0.22, 0.18)
    return jnp.clip(values, -bound, bound).astype(kind)


def setup_inputs(seed: int = 0) -> dict:
    streams_of = jax.random.split(jax.random.key(seed), 6)
    return {
        "embeddings": draw_embeddings(jax.random.fold_in(streams_of[5], 71), 0),
        "row_parent": draw_row_parent(jax.random.fold_in(streams_of[5], 71), 0),
        "block_fill": draw_block_fill(jax.random.fold_in(streams_of[5], 71), 0),
        "child_parent": draw_child_parent(jax.random.fold_in(streams_of[5], 71), 0),
        "centroids": noise(streams_of[4], (KIDS, D), 1.0, 6.0, ((0, 64),)),
    }


def expect_step(xs, tags, cent, kid_par):
    csq = jnp.sum(jnp.square(cent.astype(jnp.float32)), axis=1)
    score = (jnp.dot(xs, cent.T, preferred_element_type=jnp.float32) - 0.5 * csq[None, :]) * (D ** -0.5)
    score = jnp.where(tags[:, None] == kid_par[None, :], score, -1e30)
    top = jnp.max(score, axis=1, keepdims=True)
    expo = jnp.exp(score - top)
    total = jnp.sum(expo, axis=1, keepdims=True)
    live = tags >= 0
    resp = jnp.where(live[:, None], expo / total, 0.0).astype(jnp.bfloat16)
    lse = jnp.where(live, top[:, 0] + jnp.log(total[:, 0]), 0.0)
    return resp, lse


def reference(embeddings, row_parent, block_fill, child_parent, centroids):
    sources = N_ROW * N_NODE
    slots = jnp.arange(CAP, dtype=jnp.int32)
    live = slots[None, None, :] < block_fill[:, :, None]
    tags = jnp.where(live, row_parent.reshape(sources, N_NODE, CAP), -1)
    xs_all = jnp.moveaxis(embeddings.reshape(sources, N_NODE, CAP, D), 1, 0)
    tag_all = jnp.moveaxis(tags, 1, 0)
    kid_all = child_parent.reshape(N_NODE, KID_DEV)
    cent_all = centroids.reshape(N_NODE, KID_DEV, D)

    def owner(pieces):
        xs, tg, kid_par, cent = pieces
        xs = xs.reshape(sources * CAP, D)
        tg = tg.reshape(sources * CAP)
        lse = jnp.zeros((sources * CAP,), jnp.float32)
        for step in range(ITERS):
            resp, lse = expect_step(xs, tg, cent, kid_par)
            sums = lax.dot_general(resp, xs, (((0,), (0,)), ((), ())), preferred_element_type=jnp.float32)
            mass = jnp.sum(resp.astype(jnp.float32), axis=0)
            cent = ((sums + cent.astype(jnp.float32)) / (mass + 1.0)[:, None]).astype(jnp.bfloat16)
        return cent, lse

    cents, lses = lax.map(owner, (xs_all, tag_all, kid_all, cent_all))
    loglik = jnp.transpose(lses.reshape(N_NODE, sources, CAP), (1, 0, 2)).reshape(ROWS)
    return cents.reshape(KIDS, D), loglik
```

```python
import jax
import jax.numpy as jnp
from jax import lax
from jax.experimental import pallas as pl
from jax.experimental.pallas import tpu as pltpu
from jax.sharding import PartitionSpec as P

MESH = pl.DeviceIdType.MESH
NY, NZ, NX = 4, 8, 4
NODES = 64
CAP = 32
WIDTH = 1024
KIDS = 512
PIECE = KIDS // 4
HALF = PIECE // 2
GROUP = 8
ROWS_G = GROUP * CAP
GROUPS = NODES // GROUP
LAST = NODES - 1
ZSTEPS = (1, 7, 2, 6, 3, 5, 4, 0)


def place():
    x, n = lax.axis_index("row"), lax.axis_index("node")
    return x, n // 16, (n // 2) % NZ, n % 2


def device(x, y, z, c):
    return x, (y * NZ + z) * 2 + c


def offsets(k):
    g, i = k // GROUP, k % GROUP
    if isinstance(k, int):
        dz = ZSTEPS[i]
    else:
        h = i // 2 + 1
        dz = (h + (i % 2) * (NZ - 2 * h)) % NZ
        dz = dz * (1 - i // 7)
    v = (g + i + 2) % 8
    return v // 2, dz, v % 2


def target(k):
    x, y, z, c = place()
    d4, dz, dc = offsets(k)
    t, pz = (c + dc) % 2, (z + dz) % NZ
    px, py = (x + t * d4) % NX, (y + (1 - t) * d4) % NY
    yj = (1 - t) * py + t * px
    return device(px, py, pz, t), (yj * NZ + pz) * 2 + t


def source(k):
    x, y, z, c = place()
    d4, dz, dc = offsets(k)
    return device((x + c * (NX - d4)) % NX, (y + (1 - c) * (NY - d4)) % NY, (z + NZ - dz) % NZ, (c + dc) % 2)


def ring(d):
    x, y, z, c = place()
    return device((x + (1 - c) * d) % NX, (y + c * d) % NY, z, c)


def across(d):
    x, y, z, c = place()
    return device((x + d) % NX, y, z, c)


def down(d):
    x, y, z, c = place()
    return device(x, (y + d) % NY, z, c)


def send(src, dst, ssem, rsem, to):
    return pltpu.make_async_remote_copy(
        src_ref=src, dst_ref=dst, send_sem=ssem, recv_sem=rsem, device_id=to, device_id_type=MESH
    )


def lane():
    return lax.broadcasted_iota(jnp.int32, (1, 128), 1)


def column(row):
    r = lax.broadcasted_iota(jnp.int32, (128, 128), 0)
    q = lax.broadcasted_iota(jnp.int32, (128, 128), 1)
    return jnp.sum(jnp.where(r == q, jnp.broadcast_to(row, (128, 128)), 0.0), axis=1, keepdims=True)


def row_of(col):
    r = lax.broadcasted_iota(jnp.int32, (128, 128), 0)
    q = lax.broadcasted_iota(jnp.int32, (128, 128), 1)
    return jnp.sum(jnp.where(r == q, jnp.broadcast_to(col, (128, 128)), 0.0), axis=0, keepdims=True)


def loop(n, body):
    lax.fori_loop(0, n, lambda i, carry: (body(i), carry)[1], 0)


def kernel(
    emb, rowpar, fill, kids, cent,
    out_c, out_l,
    xs, tags, tagr, tagm, kidr, kidc, cen, csq, resp, sums, massl, massr, massg,
    snd, relay, got, fin, lsem, lsnd, lret,
    a2s, a2r, tsem, cens, cenr, kisem, rss, rsr, mss, msr, ags, agr, fws, fwr, lss, lsr, osem,
):
    x, y, z, c = place()
    r = (1 - c) * x + c * y
    served = ((1 - c) * y + c * x) * (NZ * 2) + z * 2 + c
    quarter = served % 4
    moved = c * jnp.minimum((x - y) * (x - y), 1)
    mirror = device(y, x, z, c)

    barrier = pltpu.get_barrier_semaphore()
    for k in range(LAST):
        pl.semaphore_signal(barrier, inc=1, device_id=source(k), device_id_type=MESH)
    for d in (1, 2, 3):
        pl.semaphore_signal(barrier, inc=1, device_id=ring(d), device_id_type=MESH)

    @pl.when(moved == 1)
    def _():
        pl.semaphore_signal(barrier, inc=1, device_id=mirror, device_id_type=MESH)

    for v in range(NODES // 4):
        limit = jnp.zeros((1, 128), jnp.int32)
        for q in range(4):
            limit = jnp.where(lane() // CAP == q, fill[0, 4 * v + q], limit)
        tags[v] = jnp.where(lane() % CAP < limit, rowpar[v], -1)
    sums[...] = jnp.zeros_like(sums)
    massl[...] = jnp.zeros_like(massl)

    pl.semaphore_wait(barrier, LAST + 3 + moved)

    @pl.when(moved == 1)
    def _():
        send(cent, cen.at[0], cens.at[0], cenr, mirror).start()
        send(kids, kidr, cens.at[1], kisem, mirror).start()

    @pl.when(moved == 0)
    def _():
        pltpu.make_async_copy(cent, cen.at[0], cenr).start()
        pltpu.make_async_copy(kids, kidr, kisem).start()

    def slot_copy(k):
        to, j = target(k)
        return send(emb.at[j], xs.at[k], a2s.at[k], a2r.at[k], to)

    def slot_tags(k):
        to, j = target(k)
        return send(tags.at[j // 4], tagr.at[(k % 4) * 16 + k // 4], tsem.at[0], tsem.at[1], to)

    def first(k):
        slot_tags(k).start()
        slot_copy(k).start()

    loop(LAST, first)
    own = pltpu.make_async_copy(emb.at[served], xs.at[LAST], a2r.at[LAST])
    own.start()
    tagr[LAST] = tags[served // 4]

    pltpu.make_async_copy(kids, kidr, kisem).wait()
    for p in range(4):
        kidc[p * PIECE:(p + 1) * PIECE, :] = column(kidr[p].astype(jnp.float32))
    pltpu.make_async_copy(cent, cen.at[0], cenr).wait()

    def norms(it):
        def one(p):
            at = pl.ds(pl.multiple_of(p * PIECE, PIECE), PIECE)
            csq[at, :] = (0.5 * WIDTH**-0.5) * jnp.sum(
                jnp.square(cen[it, at, :].astype(jnp.float32)), axis=1, keepdims=True
            )
        loop(4, one)

    norms(0)

    pltpu.make_async_copy(tagr.at[pl.ds(0, LAST)], tagr.at[pl.ds(0, LAST)], tsem.at[1]).wait()

    def merge(v):
        total = jnp.zeros((1, 128), jnp.int32)
        for q in range(4):
            turned = pltpu.roll(tagr[q * 16 + v], ((q + 4 - quarter) % 4) * CAP, 1)
            total = jnp.where(lane() // CAP == q, turned, total)
        tagm[v] = total.astype(jnp.float32)

    loop(NODES // 4, merge)

    def expect(it, g):
        rows = xs[pl.ds(g * GROUP, GROUP)].reshape(ROWS_G, WIDTH)
        tag = jnp.concatenate([tagm[2 * g], tagm[2 * g + 1]], axis=1)
        score = lax.dot_general(cen[it], rows, (((1,), (1,)), ((), ())), preferred_element_type=jnp.float32)
        score = score * (WIDTH**-0.5) - csq[...]
        score = jnp.where(kidc[...] == tag, score, -1e30)
        top = jnp.max(score, axis=0, keepdims=True)
        expo = jnp.exp(score - top)
        total = jnp.sum(expo, axis=0, keepdims=True)
        live = tag >= 0.0
        weight = (expo * jnp.where(live, 1.0 / total, 0.0)).astype(jnp.bfloat16)
        return rows, weight, jnp.where(live, top + jnp.log(total), 0.0)

    def add_mass(weight):
        wide = weight.astype(jnp.float32)
        massl[...] += wide[:, :128] + wide[:, 128:]

    def group_one(g):
        def arrived(i):
            pltpu.make_async_copy(emb.at[0], xs.at[g * GROUP + i], a2r.at[g * GROUP + i]).wait()

        loop(GROUP, arrived)
        rows, weight, _ = expect(0, g)
        sums[...] += jnp.dot(weight, rows, preferred_element_type=jnp.float32)
        add_mass(weight)

    loop(GROUPS, group_one)

    def piece(d):
        return pl.ds(pl.multiple_of(((r + d) % 4) * PIECE, PIECE), PIECE)

    def part(d, h):
        return pl.ds(pl.multiple_of(((r + d) % 4) * PIECE + h * HALF, HALF), HALF)

    def half(h):
        return pl.ds(h * HALF, HALF)

    def reduce_scatter(it, before):
        right, left = ring(1), ring(3)
        before(2)
        snd[it, 0] = sums[piece(2), :].astype(jnp.bfloat16)
        far_a = send(snd.at[it, 0, half(0)], relay.at[it, 0], rss.at[it, 0], rsr.at[it, 0], right)
        far_b = send(snd.at[it, 0, half(1)], relay.at[it, 1], rss.at[it, 1], rsr.at[it, 1], left)
        far_a.start()
        far_b.start()
        before(1)
        snd[it, 1, half(1)] = sums[part(1, 1), :].astype(jnp.bfloat16)
        near_r = send(snd.at[it, 1, half(1)], got.at[it, 0, half(1)], rss.at[it, 2], rsr.at[it, 2], right)
        near_r.start()
        before(3)
        snd[it, 2, half(0)] = sums[part(3, 0), :].astype(jnp.bfloat16)
        near_l = send(snd.at[it, 2, half(0)], got.at[it, 1, half(0)], rss.at[it, 3], rsr.at[it, 3], left)
        near_l.start()
        for p in range(4):
            massr[it, p] = row_of(jnp.sum(massl[p * PIECE:(p + 1) * PIECE, :], axis=1, keepdims=True))
        masses = [
            send(massr.at[it, (r + d) % 4], massg.at[it, d - 1], mss.at[it, d - 1], msr.at[it, d - 1], ring(d))
            for d in (1, 2, 3)
        ]
        for m in masses:
            m.start()
        far_a.wait_recv()
        snd[it, 1, half(0)] = (sums[part(1, 0), :] + relay[it, 0].astype(jnp.float32)).astype(jnp.bfloat16)
        on_r = send(snd.at[it, 1, half(0)], got.at[it, 0, half(0)], rss.at[it, 4], rsr.at[it, 4], right)
        on_r.start()
        far_b.wait_recv()
        snd[it, 2, half(1)] = (sums[part(3, 1), :] + relay[it, 1].astype(jnp.float32)).astype(jnp.bfloat16)
        on_l = send(snd.at[it, 2, half(1)], got.at[it, 1, half(1)], rss.at[it, 5], rsr.at[it, 5], left)
        on_l.start()
        before(0)
        for m in masses:
            m.wait_recv()
        mass = column(massr[it, r] + massg[it, 0] + massg[it, 1] + massg[it, 2]) + 1.0
        near_r.wait_recv()
        near_l.wait_recv()
        on_r.wait_recv()
        on_l.wait_recv()
        for o in (far_a, far_b, near_r, near_l, on_r, on_l, *masses):
            o.wait_send()
        total = sums[piece(0), :] + got[it, 0].astype(jnp.float32) + got[it, 1].astype(jnp.float32)
        total = total + cen[it, piece(0), :].astype(jnp.float32)
        return (total / mass).astype(jnp.bfloat16)

    def gather(it, place_of, right, left, after):
        copies = []
        for s, (h, to) in enumerate(((0, right), (1, left), (1, right), (0, left))):
            mine = place_of(0, h)
            copies.append(send(mine, mine, ags.at[it, s], agr.at[it, s], to))
            copies[-1].start()
        after(0)
        copies[0].wait_recv()
        on_r = send(place_of(3, 0), place_of(3, 0), ags.at[it, 4], agr.at[it, 4], right)
        on_r.start()
        copies[1].wait_recv()
        on_l = send(place_of(1, 1), place_of(1, 1), ags.at[it, 5], agr.at[it, 5], left)
        on_l.start()
        copies[2].wait_recv()
        after(3)
        copies[3].wait_recv()
        after(1)
        on_r.wait_recv()
        on_l.wait_recv()
        after(2)
        for o in (*copies, on_r, on_l):
            o.wait_send()

    nothing = lambda d: None

    cen[1, piece(0), :] = reduce_scatter(0, nothing)
    gather(0, lambda d, h: cen.at[1, part(d, h)], ring(1), ring(3), nothing)

    norms(1)
    massl[...] = jnp.zeros_like(massl)

    def group_two(g):
        _, weight, lse = expect(1, g)
        resp[g] = weight
        add_mass(weight)
        lsem[2 * g] = lse[:, :128]
        lsem[2 * g + 1] = lse[:, 128:]

    loop(GROUPS, group_two)

    def turn(v):
        for q in range(4):
            lsnd[4 * v + q] = pltpu.roll(lsem[v], ((quarter + 4 - q) % 4) * CAP, 1)

    loop(NODES // 4, turn)

    def back(k):
        return send(lsnd.at[k], lret.at[served], lss, lsr, source(k))

    lret[served] = lsnd[LAST]

    def maximize(d):
        total = jnp.zeros((PIECE, WIDTH), jnp.float32)

        def one(g, total):
            rows = xs[pl.ds(g * GROUP, GROUP)].reshape(ROWS_G, WIDTH)
            return total + jnp.dot(resp[g, piece(d), :], rows, preferred_element_type=jnp.float32)

        sums[piece(d), :] = lax.fori_loop(0, GROUPS, one, total)

    mine = reduce_scatter(1, maximize)
    fin[c, x] = mine[:, :] if False else mine
    loop(LAST, lambda k: back(k).start())

    def spot(d, h):
        return fin.at[c, (x + d) % 4, half(h)]

    def swap(d):
        to = (y + d) % 4
        return send(fin.at[1, to], fin.at[0, y], fws.at[d - 1], fwr.at[d - 1], down(d))

    gather(1, spot, across(1), across(3), nothing)

    @pl.when(c == 1)
    def _():
        for d in (1, 2, 3):
            swap(d).start()
        fin[0, y] = fin[1, y]
        for d in (1, 2, 3):
            swap(d).wait_recv()
        for d in (1, 2, 3):
            swap(d).wait_send()

    out = pltpu.make_async_copy(fin.at[0], out_c, osem)
    out.start()

    pltpu.make_async_copy(lret.at[pl.ds(0, LAST)], lret.at[pl.ds(0, LAST)], lsr).wait()
    for v in range(NODES // 4):
        total = jnp.zeros((1, 128), jnp.float32)
        for q in range(4):
            total = jnp.where(lane() // CAP == q, lret[4 * v + q], total)
        out_l[v] = total

    pltpu.make_async_copy(lsnd.at[pl.ds(0, LAST)], lsnd.at[pl.ds(0, LAST)], lss).wait()
    pltpu.make_async_copy(tagr.at[pl.ds(0, LAST)], tagr.at[pl.ds(0, LAST)], tsem.at[0]).wait()
    loop(LAST, lambda k: slot_copy(k).wait_send())

    @pl.when(moved == 1)
    def _():
        send(cent, cen.at[0], cens.at[0], cenr, mirror).wait_send()
        send(kids, kidr, cens.at[1], kisem, mirror).wait_send()

    out.wait()


def body(embeddings, row_parent, block_fill, child_parent, centroids):
    any_, vmem, smem = (pl.BlockSpec(memory_space=m) for m in (pl.ANY, pltpu.VMEM, pltpu.SMEM))
    bf16, f32, i32, dma = jnp.bfloat16, jnp.float32, jnp.int32, pltpu.SemaphoreType.DMA
    cents, lse = pl.pallas_call(
        kernel,
        out_shape=(
            jax.ShapeDtypeStruct((4, PIECE, WIDTH), bf16),
            jax.ShapeDtypeStruct((NODES // 4, 1, 128), f32),
        ),
        in_specs=[any_, vmem, smem, vmem, any_],
        out_specs=(any_, vmem),
        scratch_shapes=[
            pltpu.VMEM((NODES, CAP, WIDTH), bf16),
            pltpu.VMEM((NODES // 4, 1, 128), i32),
            pltpu.VMEM((NODES, 1, 128), i32),
            pltpu.VMEM((NODES // 4, 1, 128), f32),
            pltpu.VMEM((4, 1, 128), i32),
            pltpu.VMEM((KIDS, 1), f32),
            pltpu.VMEM((2, KIDS, WIDTH), bf16),
            pltpu.VMEM((KIDS, 1), f32),
            pltpu.VMEM((GROUPS, KIDS, ROWS_G), bf16),
            pltpu.VMEM((KIDS, WIDTH), f32),
            pltpu.VMEM((KIDS, 128), f32),
            pltpu.VMEM((2, 4, 1, 128), f32),
            pltpu.VMEM((2, 3, 1, 128), f32),
            pltpu.VMEM((2, 3, PIECE, WIDTH), bf16),
            pltpu.VMEM((2, 2, HALF, WIDTH), bf16),
            pltpu.VMEM((2, 2, PIECE, WIDTH), bf16),
            pltpu.VMEM((2, 4, PIECE, WIDTH), bf16),
            pltpu.VMEM((NODES // 4, 1, 128), f32),
            pltpu.VMEM((NODES, 1, 128), f32),
            pltpu.VMEM((NODES, 1, 128), f32),
            dma((NODES,)), dma((NODES,)), dma((2,)), dma((2,)), dma, dma,
            dma((2, 6)), dma((2, 6)), dma((2, 3)), dma((2, 3)), dma((2, 6)), dma((2, 6)),
            dma((3,)), dma((3,)), dma, dma, dma,
        ],
        compiler_params=pltpu.CompilerParams(
            collective_id=1, has_side_effects=True, vmem_limit_bytes=60 * 2**20
        ),
        cost_estimate=pl.CostEstimate(flops=10**10, bytes_accessed=2**23, transcendentals=2**21),
        name="em",
    )(
        embeddings.reshape(NODES, CAP, WIDTH),
        row_parent.reshape(NODES // 4, 1, 128),
        block_fill,
        child_parent.reshape(4, 1, 128),
        centroids,
    )
    return cents.reshape(KIDS, WIDTH), lse.reshape(NODES * CAP)


def solution(mesh):
    placed = (
        P(("row", "node"), None),
        P(("row", "node")),
        P(("row", "node"), None),
        P("node"),
        P("node", None),
    )
    return jax.shard_map(
        body,
        mesh=mesh,
        in_specs=placed,
        out_specs=(P("node", None), P(("row", "node"))),
        check_vma=False,
    )
```

```python
import jax
import jax.numpy as jnp
from jax import lax
from jax.experimental import pallas as pl
from jax.experimental.pallas import tpu as pltpu
from jax.sharding import PartitionSpec as P

MESH = pl.DeviceIdType.MESH
NY, NZ, NX = 4, 8, 4
NODES = 64
CAP = 32
WIDTH = 1024
KIDS = 512
PIECE = KIDS // 4
HALF = PIECE // 2
GROUP = 8
ROWS_G = GROUP * CAP
GROUPS = NODES // GROUP
NEAR = 3
AHEAD = 3


def place():
    x, n = lax.axis_index("row"), lax.axis_index("node")
    return x, n // 16, (n // 2) % NZ, n % 2


def device(x, y, z, c):
    return x, (y * NZ + z) * 2 + c


def offsets(k):
    g, i = k // GROUP, k % GROUP
    h = (i + 1) // 2
    v = (g + i) % 8
    return v // 2, (h + (1 - i % 2) * (NZ - 2 * h)) % NZ, v % 2


def target(k):
    x, y, z, c = place()
    d4, dz, dc = offsets(k)
    t, pz = (c + dc) % 2, (z + dz) % NZ
    px, py = (x + t * d4) % NX, (y + (1 - t) * d4) % NY
    yj = (1 - t) * py + t * px
    return device(px, py, pz, t), (yj * NZ + pz) * 2 + t


def source(k):
    x, y, z, c = place()
    d4, dz, dc = offsets(k)
    return device((x + c * (NX - d4)) % NX, (y + (1 - c) * (NY - d4)) % NY, (z + NZ - dz) % NZ, (c + dc) % 2)


def ring(d):
    x, y, z, c = place()
    return device((x + (1 - c) * d) % NX, (y + c * d) % NY, z, c)


def across(d):
    x, y, z, c = place()
    return device((x + d) % NX, y, z, c)


def along(d):
    x, y, z, c = place()
    return device(x, y, (z + d) % NZ, c)


def down(d):
    x, y, z, c = place()
    return device(x, (y + d) % NY, z, c)


def send(src, dst, ssem, rsem, to):
    return pltpu.make_async_remote_copy(
        src_ref=src, dst_ref=dst, send_sem=ssem, recv_sem=rsem, device_id=to, device_id_type=MESH
    )


def lane():
    return lax.broadcasted_iota(jnp.int32, (1, 128), 1)


def column(row):
    r = lax.broadcasted_iota(jnp.int32, (128, 128), 0)
    q = lax.broadcasted_iota(jnp.int32, (128, 128), 1)
    return jnp.sum(jnp.where(r == q, jnp.broadcast_to(row, (128, 128)), 0.0), axis=1, keepdims=True)


def row_of(col):
    r = lax.broadcasted_iota(jnp.int32, (128, 128), 0)
    q = lax.broadcasted_iota(jnp.int32, (128, 128), 1)
    return jnp.sum(jnp.where(r == q, jnp.broadcast_to(col, (128, 128)), 0.0), axis=0, keepdims=True)


def loop(n, body):
    lax.fori_loop(0, n, lambda i, carry: (body(i), carry)[1], 0)


def kernel(
    emb, rowpar, fill, kids, cent,
    out_c, out_l,
    xs, tags, tagr, tagm, kidr, kidc, cen, csq, resp, sums, massl, massr, massg,
    snd, relay, got, fin, lsem, lsnd, lret,
    a2s, a2r, tags_s, tags_r, cens, cenr, kisem, rss, rsr, mss, msr, ags, agr, fws, fwr, lss, lsr, stage, stage_out, lout_sem,
):
    x, y, z, c = place()
    r = (1 - c) * x + c * y
    served = ((1 - c) * y + c * x) * (NZ * 2) + z * 2 + c
    quarter = served % 4
    moved = c * jnp.minimum((x - y) * (x - y), 1)
    mirror = device(y, x, z, c)

    barrier = pltpu.get_barrier_semaphore()
    for k in range(1, NODES):
        if k % GROUP < NEAR:
            pl.semaphore_signal(barrier, inc=1, device_id=source(k), device_id_type=MESH)
    for d in (1, 2, 3):
        pl.semaphore_signal(barrier, inc=1, device_id=ring(d), device_id_type=MESH)

    @pl.when(moved == 1)
    def _():
        pl.semaphore_signal(barrier, inc=1, device_id=mirror, device_id_type=MESH)

    for v in range(NODES // 4):
        limit = jnp.zeros((1, 128), jnp.int32)
        for q in range(4):
            limit = jnp.where(lane() // CAP == q, fill[0, 4 * v + q], limit)
        tags[v] = jnp.where(lane() % CAP < limit, rowpar[v], -1)
    sums[...] = jnp.zeros_like(sums)
    massl[...] = jnp.zeros_like(massl)

    pl.semaphore_wait(barrier, NEAR * GROUPS - 1 + 3 + moved)

    @pl.when(moved == 1)
    def _():
        send(cent, cen.at[0], cens.at[0], cenr, mirror).start()
        send(kids, kidr, cens.at[1], kisem, mirror).start()

    @pl.when(moved == 0)
    def _():
        pltpu.make_async_copy(cent, cen.at[0], cenr).start()
        pltpu.make_async_copy(kids, kidr, kisem).start()

    def slot_copy(k):
        to, j = target(k)
        return send(emb.at[j], xs.at[k], a2s.at[k], a2r.at[k], to)

    def slot_tags(k):
        to, j = target(k)
        return send(tags.at[j // 4], tagr.at[k], tags_s, tags_r.at[k // GROUP], to)

    def start(k):
        slot_tags(k).start()
        slot_copy(k).start()

    def start_group(g):
        loop(GROUP, lambda i: start(g * GROUP + GROUP - 1 - i))

    def tell(s):
        for d in (1, NZ - 1):
            pl.semaphore_signal(stage.at[s], inc=1, device_id=along(d), device_id_type=MESH)

    tell(0)
    loop(NEAR - 1, lambda j: start(j + 1))
    loop(NEAR * (AHEAD - 1), lambda j: start((1 + j // NEAR) * GROUP + j % NEAR))
    own = pltpu.make_async_copy(emb.at[served], xs.at[0], a2r.at[0])
    own.start()
    own_tags = pltpu.make_async_copy(tags.at[served // 4], tagr.at[0], tags_r.at[0])
    own_tags.start()
    pl.semaphore_wait(stage.at[0], 2)
    tell(1)
    pl.semaphore_wait(stage.at[1], 2)
    tell(2)
    pl.semaphore_wait(stage.at[2], 2)
    n = GROUP - NEAR
    loop(AHEAD * n, lambda j: start((j // n) * GROUP + GROUP - 1 - j % n))

    pltpu.make_async_copy(kids, kidr, kisem).wait()
    for p in range(4):
        kidc[p * PIECE:(p + 1) * PIECE, :] = column(kidr[p].astype(jnp.float32))
    pltpu.make_async_copy(cent, cen.at[0], cenr).wait()

    def norms(it):
        def one(p):
            at = pl.ds(pl.multiple_of(p * PIECE, PIECE), PIECE)
            csq[at, :] = (0.5 * WIDTH**-0.5) * jnp.sum(
                jnp.square(cen[it, at, :].astype(jnp.float32)), axis=1, keepdims=True
            )
        loop(4, one)

    norms(0)

    def merge(v):
        total = jnp.zeros((1, 128), jnp.int32)
        for q in range(4):
            turned = pltpu.roll(tagr[4 * v + q], ((q + 4 - quarter) % 4) * CAP, 1)
            total = jnp.where(lane() // CAP == q, turned, total)
        tagm[v] = total.astype(jnp.float32)

    def expect(it, g):
        rows = xs[pl.ds(g * GROUP, GROUP)].reshape(ROWS_G, WIDTH)
        tag = jnp.concatenate([tagm[2 * g], tagm[2 * g + 1]], axis=1)
        score = lax.dot_general(cen[it], rows, (((1,), (1,)), ((), ())), preferred_element_type=jnp.float32)
        score = score * (WIDTH**-0.5) - csq[...]
        score = jnp.where(kidc[...] == tag, score, -1e30)
        top = jnp.max(score, axis=0, keepdims=True)
        expo = jnp.exp(score - top)
        total = jnp.sum(expo, axis=0, keepdims=True)
        live = tag >= 0.0
        weight = (expo * jnp.where(live, 1.0 / total, 0.0)).astype(jnp.bfloat16)
        return rows, weight, jnp.where(live, top + jnp.log(total), 0.0)

    def add_mass(weight):
        wide = weight.astype(jnp.float32)
        massl[...] += wide[:, :128] + wide[:, 128:]

    def group_one(g):
        def arrived(i):
            pltpu.make_async_copy(emb.at[0], xs.at[g * GROUP + i], a2r.at[g * GROUP + i]).wait()

        loop(GROUP, arrived)

        @pl.when(g + AHEAD < GROUPS)
        def _():
            start_group(g + AHEAD)

        group_tags = tagr.at[pl.ds(g * GROUP, GROUP)]
        pltpu.make_async_copy(group_tags, group_tags, tags_r.at[g]).wait()
        merge(2 * g)
        merge(2 * g + 1)
        rows, weight, _ = expect(0, g)
        sums[...] += jnp.dot(weight, rows, preferred_element_type=jnp.float32)
        add_mass(weight)

    loop(GROUPS, group_one)

    def piece(d):
        return pl.ds(pl.multiple_of(((r + d) % 4) * PIECE, PIECE), PIECE)

    def part(d, h):
        return pl.ds(pl.multiple_of(((r + d) % 4) * PIECE + h * HALF, HALF), HALF)

    def half(h):
        return pl.ds(h * HALF, HALF)

    def reduce_scatter(it, before, meanwhile):
        right, left = ring(1), ring(3)
        before(2)
        snd[it, 0] = sums[piece(2), :].astype(jnp.bfloat16)
        far_a = send(snd.at[it, 0, half(0)], relay.at[it, 0], rss.at[it, 0], rsr.at[it, 0], right)
        far_b = send(snd.at[it, 0, half(1)], relay.at[it, 1], rss.at[it, 1], rsr.at[it, 1], left)
        far_a.start()
        far_b.start()
        before(1)
        snd[it, 1, half(1)] = sums[part(1, 1), :].astype(jnp.bfloat16)
        near_r = send(snd.at[it, 1, half(1)], got.at[it, 0, half(1)], rss.at[it, 2], rsr.at[it, 2], right)
        near_r.start()
        before(3)
        snd[it, 2, half(0)] = sums[part(3, 0), :].astype(jnp.bfloat16)
        near_l = send(snd.at[it, 2, half(0)], got.at[it, 1, half(0)], rss.at[it, 3], rsr.at[it, 3], left)
        near_l.start()
        for p in range(4):
            massr[it, p] = row_of(jnp.sum(massl[p * PIECE:(p + 1) * PIECE, :], axis=1, keepdims=True))
        masses = [
            send(massr.at[it, (r + d) % 4], massg.at[it, d - 1], mss.at[it, d - 1], msr.at[it, d - 1], ring(d))
            for d in (1, 2, 3)
        ]
        for m in masses:
            m.start()
        far_a.wait_recv()
        snd[it, 1, half(0)] = (sums[part(1, 0), :] + relay[it, 0].astype(jnp.float32)).astype(jnp.bfloat16)
        on_r = send(snd.at[it, 1, half(0)], got.at[it, 0, half(0)], rss.at[it, 4], rsr.at[it, 4], right)
        on_r.start()
        far_b.wait_recv()
        snd[it, 2, half(1)] = (sums[part(3, 1), :] + relay[it, 1].astype(jnp.float32)).astype(jnp.bfloat16)
        on_l = send(snd.at[it, 2, half(1)], got.at[it, 1, half(1)], rss.at[it, 5], rsr.at[it, 5], left)
        on_l.start()
        before(0)
        meanwhile()
        for m in masses:
            m.wait_recv()
        mass = column(massr[it, r] + massg[it, 0] + massg[it, 1] + massg[it, 2]) + 1.0
        near_r.wait_recv()
        near_l.wait_recv()
        on_r.wait_recv()
        on_l.wait_recv()
        for o in (far_a, far_b, near_r, near_l, on_r, on_l, *masses):
            o.wait_send()
        total = sums[piece(0), :] + got[it, 0].astype(jnp.float32) + got[it, 1].astype(jnp.float32)
        total = total + cen[it, piece(0), :].astype(jnp.float32)
        return (total / mass).astype(jnp.bfloat16)

    def gather(it, place_of, right, left, after):
        copies = []
        for s, (h, to) in enumerate(((0, right), (1, left), (1, right), (0, left))):
            mine = place_of(0, h)
            copies.append(send(mine, mine, ags.at[it, s], agr.at[it, s], to))
            copies[-1].start()
        after(0)
        copies[0].wait_recv()
        on_r = send(place_of(3, 0), place_of(3, 0), ags.at[it, 4], agr.at[it, 4], right)
        on_r.start()
        copies[1].wait_recv()
        on_l = send(place_of(1, 1), place_of(1, 1), ags.at[it, 5], agr.at[it, 5], left)
        on_l.start()
        copies[2].wait_recv()
        after(3)
        copies[3].wait_recv()
        after(1)
        on_r.wait_recv()
        on_l.wait_recv()
        after(2)
        for o in (*copies, on_r, on_l):
            o.wait_send()

    nothing = lambda d: None

    cen[1, piece(0), :] = reduce_scatter(0, nothing, lambda: None)
    gather(0, lambda d, h: cen.at[1, part(d, h)], ring(1), ring(3), nothing)

    norms(1)
    massl[...] = jnp.zeros_like(massl)

    def group_two(g):
        _, weight, lse = expect(1, g)
        resp[g] = weight
        add_mass(weight)
        lsem[2 * g] = lse[:, :128]
        lsem[2 * g + 1] = lse[:, 128:]

    loop(GROUPS, group_two)

    def turn(v):
        for q in range(4):
            lsnd[4 * v + q] = pltpu.roll(lsem[v], ((quarter + 4 - q) % 4) * CAP, 1)

    def back(k):
        return send(lsnd.at[k], lret.at[served], lss, lsr, source(k))

    def maximize(d):
        total = jnp.zeros((PIECE, WIDTH), jnp.float32)

        def one(g, total):
            rows = xs[pl.ds(g * GROUP, GROUP)].reshape(ROWS_G, WIDTH)
            return total + jnp.dot(resp[g, piece(d), :], rows, preferred_element_type=jnp.float32)

        sums[piece(d), :] = lax.fori_loop(0, GROUPS, one, total)

    def turn_all():
        loop(NODES // 4, turn)
        lret[served] = lsnd[0]

    fin[c, x] = reduce_scatter(1, maximize, turn_all)

    def spot(d, h):
        return fin.at[c, (x + d) % 4, half(h)]

    def swap(w):
        return send(fin.at[1, w], fin.at[0, y], fws.at[w], fwr.at[y], device(x, w, z, c))

    def pass_on(d):
        w = (x + d) % 4

        @pl.when(c * (w - y) != 0)
        def _():
            swap(w).start()

        @pl.when(c * (1 + (w - y) * (w - y)) == 1)
        def _():
            fin[0, y] = fin[1, y]

        if d == 0:
            loop(NODES - 1, lambda k: back(k + 1).start())

    gather(1, spot, across(1), across(3), pass_on)

    @pl.when(c == 1)
    def _():
        for d in (1, 2, 3):
            w = (y + d) % 4
            pltpu.make_async_copy(fin.at[1, w], fin.at[0, w], fwr.at[w]).wait()
        for d in (1, 2, 3):
            swap((y + d) % 4).wait_send()

    out = pltpu.make_async_copy(fin.at[0], out_c, stage_out)
    out.start()

    pltpu.make_async_copy(lret.at[pl.ds(1, NODES - 1)], lret.at[pl.ds(1, NODES - 1)], lsr).wait()
    for v in range(NODES // 4):
        total = jnp.zeros((1, 128), jnp.float32)
        for q in range(4):
            total = jnp.where(lane() // CAP == q, lret[4 * v + q], total)
        lsem[v] = total

    pltpu.make_async_copy(lsnd.at[pl.ds(1, NODES - 1)], lsnd.at[pl.ds(1, NODES - 1)], lss).wait()
    pltpu.make_async_copy(tagr.at[pl.ds(1, NODES - 1)], tagr.at[pl.ds(1, NODES - 1)], tags_s).wait()
    loop(NODES - 1, lambda k: slot_copy(k + 1).wait_send())

    @pl.when(moved == 1)
    def _():
        send(cent, cen.at[0], cens.at[0], cenr, mirror).wait_send()
        send(kids, kidr, cens.at[1], kisem, mirror).wait_send()

    lout = pltpu.make_async_copy(lsem, out_l, lout_sem)
    lout.start()
    lout.wait()
    out.wait()


def put(cents, lse, out_c, out_l, held, held_l, isem, osem):
    into = [pltpu.make_async_copy(cents.at[i], held.at[i], isem.at[i]) for i in range(4)]
    into.append(pltpu.make_async_copy(lse, held_l, isem.at[4]))
    out = [pltpu.make_async_copy(held.at[i], out_c.at[i], osem.at[i]) for i in range(4)]
    out.append(pltpu.make_async_copy(held_l, out_l, osem.at[4]))
    for o in into:
        o.start()
    for i, o in zip(into, out):
        i.wait()
        o.start()
    for o in out:
        o.wait()


def body(embeddings, row_parent, block_fill, child_parent, centroids):
    any_, vmem, smem = (pl.BlockSpec(memory_space=m) for m in (pl.ANY, pltpu.VMEM, pltpu.SMEM))
    bf16, f32, i32, dma = jnp.bfloat16, jnp.float32, jnp.int32, pltpu.SemaphoreType.DMA
    cents, lse = pl.pallas_call(
        kernel,
        out_shape=(
            jax.ShapeDtypeStruct((4, PIECE, WIDTH), bf16),
            jax.ShapeDtypeStruct((NODES // 4, 1, 128), f32),
        ),
        in_specs=[any_, vmem, smem, vmem, any_],
        out_specs=(any_, any_),
        scratch_shapes=[
            pltpu.VMEM((NODES, CAP, WIDTH), bf16),
            pltpu.VMEM((NODES // 4, 1, 128), i32),
            pltpu.VMEM((NODES, 1, 128), i32),
            pltpu.VMEM((NODES // 4, 1, 128), f32),
            pltpu.VMEM((4, 1, 128), i32),
            pltpu.VMEM((KIDS, 1), f32),
            pltpu.VMEM((2, KIDS, WIDTH), bf16),
            pltpu.VMEM((KIDS, 1), f32),
            pltpu.VMEM((GROUPS, KIDS, ROWS_G), bf16),
            pltpu.VMEM((KIDS, WIDTH), f32),
            pltpu.VMEM((KIDS, 128), f32),
            pltpu.VMEM((2, 4, 1, 128), f32),
            pltpu.VMEM((2, 3, 1, 128), f32),
            pltpu.VMEM((2, 3, PIECE, WIDTH), bf16),
            pltpu.VMEM((2, 2, HALF, WIDTH), bf16),
            pltpu.VMEM((2, 2, PIECE, WIDTH), bf16),
            pltpu.VMEM((2, 4, PIECE, WIDTH), bf16),
            pltpu.VMEM((NODES // 4, 1, 128), f32),
            pltpu.VMEM((NODES, 1, 128), f32),
            pltpu.VMEM((NODES, 1, 128), f32),
            dma((NODES,)), dma((NODES,)), dma, dma((GROUPS,)), dma((2,)), dma, dma,
            dma((2, 6)), dma((2, 6)), dma((2, 3)), dma((2, 3)), dma((2, 6)), dma((2, 6)),
            dma((4,)), dma((4,)), dma, dma, pltpu.SemaphoreType.REGULAR((3,)), dma, dma,
        ],
        compiler_params=pltpu.CompilerParams(
            collective_id=1, has_side_effects=True, vmem_limit_bytes=60 * 2**20
        ),
        cost_estimate=pl.CostEstimate(flops=10**10, bytes_accessed=2**23, transcendentals=2**21),
        name="em",
    )(
        embeddings.reshape(NODES, CAP, WIDTH),
        row_parent.reshape(NODES // 4, 1, 128),
        block_fill,
        child_parent.reshape(4, 1, 128),
        centroids,
    )
    cents, lse = pl.pallas_call(
        put,
        out_shape=(
            jax.ShapeDtypeStruct((4, PIECE, WIDTH), bf16),
            jax.ShapeDtypeStruct((NODES // 4, 1, 128), f32),
        ),
        in_specs=[any_, any_],
        out_specs=(any_, any_),
        scratch_shapes=[
            pltpu.VMEM((4, PIECE, WIDTH), bf16),
            pltpu.VMEM((NODES // 4, 1, 128), f32),
            dma((5,)),
            dma((5,)),
        ],
        compiler_params=pltpu.CompilerParams(vmem_limit_bytes=60 * 2**20),
        name="put",
    )(cents, lse)
    return cents.reshape(KIDS, WIDTH), lse.reshape(NODES * CAP)


def solution(mesh):
    placed = (
        P(("row", "node"), None),
        P(("row", "node")),
        P(("row", "node"), None),
        P("node"),
        P("node", None),
    )
    return jax.shard_map(
        body,
        mesh=mesh,
        in_specs=placed,
        out_specs=(P("node", None), P(("row", "node"))),
        check_vma=False,
    )
```

```python
import jax
import jax.numpy as jnp
from jax import lax
from jax.experimental import pallas as pl
from jax.experimental.pallas import tpu as pltpu
from jax.sharding import PartitionSpec as P

MESH = pl.DeviceIdType.MESH
NY, NZ, NX = 4, 8, 4
NODES = 64
CAP = 32
WIDTH = 1024
KIDS = 512
PIECE = KIDS // 4
HALF = PIECE // 2
GROUP = 8
ROWS_G = GROUP * CAP
GROUPS = NODES // GROUP
NEAR = 3
AHEAD = 3
POS = (0, 1, 3, 2)


def place():
    x, n = lax.axis_index("row"), lax.axis_index("node")
    return x, n // 16, (n // 2) % NZ, n % 2


def device(x, y, z, c):
    return x, (y * NZ + z) * 2 + c


def offsets(k):
    g, i = k // GROUP, k % GROUP
    h = (i + 1) // 2
    v = (g + i) % 8
    return v // 2, (h + (1 - i % 2) * (NZ - 2 * h)) % NZ, v % 2


def target(k):
    x, y, z, c = place()
    d4, dz, dc = offsets(k)
    t, pz = (c + dc) % 2, (z + dz) % NZ
    px, py = (x + t * d4) % NX, (y + (1 - t) * d4) % NY
    yj = (1 - t) * py + t * px
    return device(px, py, pz, t), (yj * NZ + pz) * 2 + t


def source(k):
    x, y, z, c = place()
    d4, dz, dc = offsets(k)
    return device((x + c * (NX - d4)) % NX, (y + (1 - c) * (NY - d4)) % NY, (z + NZ - dz) % NZ, (c + dc) % 2)


def ring(d):
    x, y, z, c = place()
    return device((x + (1 - c) * d) % NX, (y + c * d) % NY, z, c)


def across(d):
    x, y, z, c = place()
    return device((x + d) % NX, y, z, c)


def along(d):
    x, y, z, c = place()
    return device(x, y, (z + d) % NZ, c)


def down(d):
    x, y, z, c = place()
    return device(x, (y + d) % NY, z, c)


def send(src, dst, ssem, rsem, to):
    return pltpu.make_async_remote_copy(
        src_ref=src, dst_ref=dst, send_sem=ssem, recv_sem=rsem, device_id=to, device_id_type=MESH
    )


def lane():
    return lax.broadcasted_iota(jnp.int32, (1, 128), 1)


def column(row):
    r = lax.broadcasted_iota(jnp.int32, (128, 128), 0)
    q = lax.broadcasted_iota(jnp.int32, (128, 128), 1)
    return jnp.sum(jnp.where(r == q, jnp.broadcast_to(row, (128, 128)), 0.0), axis=1, keepdims=True)


def row_of(col):
    r = lax.broadcasted_iota(jnp.int32, (128, 128), 0)
    q = lax.broadcasted_iota(jnp.int32, (128, 128), 1)
    return jnp.sum(jnp.where(r == q, jnp.broadcast_to(col, (128, 128)), 0.0), axis=0, keepdims=True)


def loop(n, body):
    lax.fori_loop(0, n, lambda i, carry: (body(i), carry)[1], 0)


def kernel(
    emb, rowpar, fill, kids, cent,
    out_c, out_l,
    xs, tags, tagr, tagm, kidr, kidc, cen, csq, resp, score, sums, massl, massr, massg,
    snd, relay, got, fin, lsem, lsnd, lret,
    a2s, a2r, tags_s, tags_r, cens, cenr, kisem, rss, rsr, mss, msr, ags, agr, fws, fwr, lss, lsr, stage, stage_out, lout_sem,
):
    x, y, z, c = place()
    r = (1 - c) * x + c * y
    served = ((1 - c) * y + c * x) * (NZ * 2) + z * 2 + c
    quarter = served % 4
    moved = c * jnp.minimum((x - y) * (x - y), 1)
    mirror = device(y, x, z, c)

    barrier = pltpu.get_barrier_semaphore()
    for k in range(1, NODES):
        if k % GROUP < NEAR:
            pl.semaphore_signal(barrier, inc=1, device_id=source(k), device_id_type=MESH)
    for d in (1, 2, 3):
        pl.semaphore_signal(barrier, inc=1, device_id=ring(d), device_id_type=MESH)

    @pl.when(moved == 1)
    def _():
        pl.semaphore_signal(barrier, inc=1, device_id=mirror, device_id_type=MESH)

    for v in range(NODES // 4):
        limit = jnp.zeros((1, 128), jnp.int32)
        for q in range(4):
            limit = jnp.where(lane() // CAP == q, fill[0, 4 * v + q], limit)
        tags[v] = jnp.where(lane() % CAP < limit, rowpar[v], -1)
    sums[...] = jnp.zeros_like(sums)
    massl[...] = jnp.zeros_like(massl)

    pl.semaphore_wait(barrier, NEAR * GROUPS - 1 + 3 + moved)

    def given(d, first):
        p = (first + d) % 4
        at = pl.ds(pl.multiple_of(p * PIECE, PIECE), PIECE)
        return (cent.at[at], cen.at[0, pl.ds(POS[d] * PIECE, PIECE)]), (kids.at[p], kidr.at[POS[d]])

    def to_mirror():
        return [
            send(src, dst, cens.at[i], sem, mirror)
            for d in range(4)
            for i, ((src, dst), sem) in enumerate(zip(given(d, x), (cenr, kisem)))
        ]

    @pl.when(moved == 1)
    def _():
        for o in to_mirror():
            o.start()

    @pl.when(moved == 0)
    def _():
        for d in range(4):
            for (src, dst), sem in zip(given(d, r), (cenr, kisem)):
                pltpu.make_async_copy(src, dst, sem).start()

    def slot_copy(k):
        to, j = target(k)
        return send(emb.at[j], xs.at[k], a2s.at[k], a2r.at[k], to)

    def slot_tags(k):
        to, j = target(k)
        return send(tags.at[j // 4], tagr.at[k], tags_s, tags_r.at[k // GROUP], to)

    def start(k):
        slot_tags(k).start()
        slot_copy(k).start()

    def start_group(g):
        loop(GROUP, lambda i: start(g * GROUP + GROUP - 1 - i))

    def tell(s):
        for d in (1, NZ - 1):
            pl.semaphore_signal(stage.at[s], inc=1, device_id=along(d), device_id_type=MESH)

    tell(0)
    loop(NEAR - 1, lambda j: start(j + 1))
    loop(NEAR * (AHEAD - 1), lambda j: start((1 + j // NEAR) * GROUP + j % NEAR))
    own = pltpu.make_async_copy(emb.at[served], xs.at[0], a2r.at[0])
    own.start()
    own_tags = pltpu.make_async_copy(tags.at[served // 4], tagr.at[0], tags_r.at[0])
    own_tags.start()
    pl.semaphore_wait(stage.at[0], 2)
    tell(1)
    pl.semaphore_wait(stage.at[1], 2)
    tell(2)
    pl.semaphore_wait(stage.at[2], 2)
    n = GROUP - NEAR
    loop(AHEAD * n, lambda j: start((j // n) * GROUP + GROUP - 1 - j % n))

    pltpu.make_async_copy(kids, kidr, kisem).wait()
    for p in range(4):
        kidc[p * PIECE:(p + 1) * PIECE, :] = column(kidr[p].astype(jnp.float32))
    pltpu.make_async_copy(cent, cen.at[0], cenr).wait()

    def norms(it, at):
        csq[at, :] = (0.5 * WIDTH**-0.5) * jnp.sum(
            jnp.square(cen[it, at, :].astype(jnp.float32)), axis=1, keepdims=True
        )

    loop(4, lambda p: norms(0, pl.ds(pl.multiple_of(p * PIECE, PIECE), PIECE)))

    def merge(v):
        total = jnp.zeros((1, 128), jnp.int32)
        for q in range(4):
            turned = pltpu.roll(tagr[4 * v + q], ((q + 4 - quarter) % 4) * CAP, 1)
            total = jnp.where(lane() // CAP == q, turned, total)
        tagm[v] = total.astype(jnp.float32)

    def rows_of(g):
        return xs[pl.ds(g * GROUP, GROUP)].reshape(ROWS_G, WIDTH)

    def products(children, rows):
        return lax.dot_general(children, rows, (((1,), (1,)), ((), ())), preferred_element_type=jnp.float32)

    def soften(g, dots):
        tag = jnp.concatenate([tagm[2 * g], tagm[2 * g + 1]], axis=1)
        score = dots * (WIDTH**-0.5) - csq[...]
        score = jnp.where(kidc[...] == tag, score, -1e30)
        top = jnp.max(score, axis=0, keepdims=True)
        expo = jnp.exp(score - top)
        total = jnp.sum(expo, axis=0, keepdims=True)
        live = tag >= 0.0
        weight = (expo * jnp.where(live, 1.0 / total, 0.0)).astype(jnp.bfloat16)
        return weight, jnp.where(live, top + jnp.log(total), 0.0)

    def add_mass(weight):
        wide = weight.astype(jnp.float32)
        massl[...] += wide[:, :128] + wide[:, 128:]

    def group_one(g):
        def arrived(i):
            pltpu.make_async_copy(emb.at[0], xs.at[g * GROUP + i], a2r.at[g * GROUP + i]).wait()

        loop(GROUP, arrived)

        @pl.when(g + AHEAD < GROUPS)
        def _():
            start_group(g + AHEAD)

        group_tags = tagr.at[pl.ds(g * GROUP, GROUP)]
        pltpu.make_async_copy(group_tags, group_tags, tags_r.at[g]).wait()
        merge(2 * g)
        merge(2 * g + 1)
        rows = rows_of(g)
        weight, _ = soften(g, products(cen[0], rows))
        sums[...] += jnp.dot(weight, rows, preferred_element_type=jnp.float32)
        add_mass(weight)

    loop(GROUPS, group_one)

    def piece(d):
        return pl.ds(POS[d % 4] * PIECE, PIECE)

    def part(d, h):
        return pl.ds(POS[d % 4] * PIECE + h * HALF, HALF)

    def half(h):
        return pl.ds(h * HALF, HALF)

    def reduce_scatter(it, before, meanwhile):
        right, left = ring(1), ring(3)
        before(2)
        snd[it, 0] = sums[piece(2), :].astype(jnp.bfloat16)
        far_a = send(snd.at[it, 0, half(0)], relay.at[it, 0], rss.at[it, 0], rsr.at[it, 0], right)
        far_b = send(snd.at[it, 0, half(1)], relay.at[it, 1], rss.at[it, 1], rsr.at[it, 1], left)
        far_a.start()
        far_b.start()
        before(1)
        snd[it, 1, half(1)] = sums[part(1, 1), :].astype(jnp.bfloat16)
        near_r = send(snd.at[it, 1, half(1)], got.at[it, 0, half(1)], rss.at[it, 2], rsr.at[it, 2], right)
        near_r.start()
        before(3)
        snd[it, 2, half(0)] = sums[part(3, 0), :].astype(jnp.bfloat16)
        near_l = send(snd.at[it, 2, half(0)], got.at[it, 1, half(0)], rss.at[it, 3], rsr.at[it, 3], left)
        near_l.start()
        for p in range(4):
            massr[it, p] = row_of(jnp.sum(massl[p * PIECE:(p + 1) * PIECE, :], axis=1, keepdims=True))
        masses = [
            send(massr.at[it, POS[d]], massg.at[it, d - 1], mss.at[it, d - 1], msr.at[it, d - 1], ring(d))
            for d in (1, 2, 3)
        ]
        for m in masses:
            m.start()
        far_a.wait_recv()
        snd[it, 1, half(0)] = (sums[part(1, 0), :] + relay[it, 0].astype(jnp.float32)).astype(jnp.bfloat16)
        on_r = send(snd.at[it, 1, half(0)], got.at[it, 0, half(0)], rss.at[it, 4], rsr.at[it, 4], right)
        on_r.start()
        far_b.wait_recv()
        snd[it, 2, half(1)] = (sums[part(3, 1), :] + relay[it, 1].astype(jnp.float32)).astype(jnp.bfloat16)
        on_l = send(snd.at[it, 2, half(1)], got.at[it, 1, half(1)], rss.at[it, 5], rsr.at[it, 5], left)
        on_l.start()
        before(0)
        meanwhile()
        for m in masses:
            m.wait_recv()
        mass = 1.0 / (column(massr[it, 0] + massg[it, 0] + massg[it, 1] + massg[it, 2]) + 1.0)
        near_r.wait_recv()
        near_l.wait_recv()
        on_r.wait_recv()
        on_l.wait_recv()
        for o in (far_a, far_b, near_r, near_l, on_r, on_l, *masses):
            o.wait_send()
        total = sums[piece(0), :] + got[it, 0].astype(jnp.float32) + got[it, 1].astype(jnp.float32)
        total = total + cen[it, piece(0), :].astype(jnp.float32)
        return (total * mass).astype(jnp.bfloat16)

    def gather(it, spot, turn, right, left, after):
        copies = []
        for s, (h, to, step) in enumerate(((0, right, -1), (1, left, 1), (1, right, -1), (0, left, 1))):
            copies.append(send(spot(0, h), spot(turn * step, h), ags.at[it, s], agr.at[it, s], to))
            copies[-1].start()
        after(0)
        copies[0].wait_recv()
        on_r = send(spot(3, 0), spot(3 - turn, 0), ags.at[it, 4], agr.at[it, 4], right)
        on_r.start()
        copies[1].wait_recv()
        on_l = send(spot(1, 1), spot(1 + turn, 1), ags.at[it, 5], agr.at[it, 5], left)
        on_l.start()
        copies[2].wait_recv()
        after(3)
        copies[3].wait_recv()
        after(1)
        on_r.wait_recv()
        on_l.wait_recv()
        after(2)
        for o in (*copies, on_r, on_l):
            o.wait_send()

    nothing = lambda d: None

    cen[1, piece(0), :] = reduce_scatter(0, nothing, lambda: None)

    massl[...] = jnp.zeros_like(massl)

    def score_new(d):
        if d == 3:
            return
        at = {0: pl.ds(0, PIECE), 1: pl.ds(PIECE, 2 * PIECE), 2: pl.ds(3 * PIECE, PIECE)}[d]
        norms(1, at)

        score[at, :] = products(cen[1, at, :], xs[...].reshape(NODES * CAP, WIDTH))

    gather(0, lambda d, h: cen.at[1, part(d, h)], 1, ring(1), ring(3), score_new)

    def group_two(g):
        weight, lse = soften(g, score[:, pl.ds(pl.multiple_of(g * ROWS_G, ROWS_G), ROWS_G)])
        resp[:, pl.ds(pl.multiple_of(g * ROWS_G, ROWS_G), ROWS_G)] = weight
        add_mass(weight)
        lsem[2 * g] = lse[:, :128]
        lsem[2 * g + 1] = lse[:, 128:]

    loop(GROUPS, group_two)

    def turn(v):
        for q in range(4):
            lsnd[4 * v + q] = pltpu.roll(lsem[v], ((quarter + 4 - q) % 4) * CAP, 1)

    def back(k):
        return send(lsnd.at[k], lret.at[served], lss, lsr, source(k))

    def maximize(d):
        if d == 3:
            return
        at, n = {0: (0, PIECE), 1: (PIECE, 2 * PIECE), 2: (3 * PIECE, PIECE)}[d]

        every = xs[...].reshape(NODES * CAP, WIDTH)
        sums[pl.ds(at, n), :] = jnp.dot(resp[pl.ds(at, n), :], every, preferred_element_type=jnp.float32)

    def turn_all():
        loop(NODES // 4, turn)
        lret[served] = lsnd[0]

    fin[c, x] = reduce_scatter(1, maximize, turn_all)

    def spot(d, h):
        return fin.at[c, (x + d) % 4, half(h)]

    def swap(w):
        return send(fin.at[1, w], fin.at[0, y], fws.at[w], fwr.at[y], device(x, w, z, c))

    def pass_on(d):
        w = (x + d) % 4

        @pl.when(c * (w - y) != 0)
        def _():
            swap(w).start()

        @pl.when(c * (1 + (w - y) * (w - y)) == 1)
        def _():
            fin[0, y] = fin[1, y]

        if d == 0:
            loop(NODES - 1, lambda k: back(k + 1).start())

    gather(1, spot, 0, across(1), across(3), pass_on)

    @pl.when(c == 1)
    def _():
        for d in (1, 2, 3):
            w = (y + d) % 4
            pltpu.make_async_copy(fin.at[1, w], fin.at[0, w], fwr.at[w]).wait()
        for d in (1, 2, 3):
            swap((y + d) % 4).wait_send()

    out = pltpu.make_async_copy(fin.at[0], out_c, stage_out)
    out.start()

    pltpu.make_async_copy(lret.at[pl.ds(1, NODES - 1)], lret.at[pl.ds(1, NODES - 1)], lsr).wait()
    for v in range(NODES // 4):
        total = jnp.zeros((1, 128), jnp.float32)
        for q in range(4):
            total = jnp.where(lane() // CAP == q, lret[4 * v + q], total)
        lsem[v] = total

    pltpu.make_async_copy(lsnd.at[pl.ds(1, NODES - 1)], lsnd.at[pl.ds(1, NODES - 1)], lss).wait()
    pltpu.make_async_copy(tagr.at[pl.ds(1, NODES - 1)], tagr.at[pl.ds(1, NODES - 1)], tags_s).wait()
    loop(NODES - 1, lambda k: slot_copy(k + 1).wait_send())

    @pl.when(moved == 1)
    def _():
        pltpu.make_async_copy(cent, cen.at[0], cens.at[0]).wait()
        pltpu.make_async_copy(kids, kidr, cens.at[1]).wait()

    lout = pltpu.make_async_copy(lsem, out_l, lout_sem)
    lout.start()
    lout.wait()
    out.wait()


def put(cents, lse, out_c, out_l, held, held_l, isem, osem):
    into = [pltpu.make_async_copy(cents.at[i], held.at[i], isem.at[i]) for i in range(4)]
    into.append(pltpu.make_async_copy(lse, held_l, isem.at[4]))
    out = [pltpu.make_async_copy(held.at[i], out_c.at[i], osem.at[i]) for i in range(4)]
    out.append(pltpu.make_async_copy(held_l, out_l, osem.at[4]))
    for o in into:
        o.start()
    for i, o in zip(into, out):
        i.wait()
        o.start()
    for o in out:
        o.wait()


def body(embeddings, row_parent, block_fill, child_parent, centroids):
    any_, vmem, smem = (pl.BlockSpec(memory_space=m) for m in (pl.ANY, pltpu.VMEM, pltpu.SMEM))
    bf16, f32, i32, dma = jnp.bfloat16, jnp.float32, jnp.int32, pltpu.SemaphoreType.DMA
    cents, lse = pl.pallas_call(
        kernel,
        out_shape=(
            jax.ShapeDtypeStruct((4, PIECE, WIDTH), bf16),
            jax.ShapeDtypeStruct((NODES // 4, 1, 128), f32),
        ),
        in_specs=[any_, vmem, smem, vmem, any_],
        out_specs=(any_, any_),
        scratch_shapes=[
            pltpu.VMEM((NODES, CAP, WIDTH), bf16),
            pltpu.VMEM((NODES // 4, 1, 128), i32),
            pltpu.VMEM((NODES, 1, 128), i32),
            pltpu.VMEM((NODES // 4, 1, 128), f32),
            pltpu.VMEM((4, 1, 128), i32),
            pltpu.VMEM((KIDS, 1), f32),
            pltpu.VMEM((2, KIDS, WIDTH), bf16),
            pltpu.VMEM((KIDS, 1), f32),
            pltpu.VMEM((KIDS, NODES * CAP), bf16),
            pltpu.VMEM((KIDS, NODES * CAP), f32),
            pltpu.VMEM((KIDS, WIDTH), f32),
            pltpu.VMEM((KIDS, 128), f32),
            pltpu.VMEM((2, 4, 1, 128), f32),
            pltpu.VMEM((2, 3, 1, 128), f32),
            pltpu.VMEM((2, 3, PIECE, WIDTH), bf16),
            pltpu.VMEM((2, 2, HALF, WIDTH), bf16),
            pltpu.VMEM((2, 2, PIECE, WIDTH), bf16),
            pltpu.VMEM((2, 4, PIECE, WIDTH), bf16),
            pltpu.VMEM((NODES // 4, 1, 128), f32),
            pltpu.VMEM((NODES, 1, 128), f32),
            pltpu.VMEM((NODES, 1, 128), f32),
            dma((NODES,)), dma((NODES,)), dma, dma((GROUPS,)), dma((2,)), dma, dma,
            dma((2, 6)), dma((2, 6)), dma((2, 3)), dma((2, 3)), dma((2, 6)), dma((2, 6)),
            dma((4,)), dma((4,)), dma, dma, pltpu.SemaphoreType.REGULAR((3,)), dma, dma,
        ],
        compiler_params=pltpu.CompilerParams(
            collective_id=1, has_side_effects=True, vmem_limit_bytes=60 * 2**20
        ),
        cost_estimate=pl.CostEstimate(flops=10**10, bytes_accessed=2**23, transcendentals=2**21),
        name="em",
    )(
        embeddings.reshape(NODES, CAP, WIDTH),
        row_parent.reshape(NODES // 4, 1, 128),
        block_fill,
        child_parent.reshape(4, 1, 128),
        centroids,
    )
    cents, lse = pl.pallas_call(
        put,
        out_shape=(
            jax.ShapeDtypeStruct((4, PIECE, WIDTH), bf16),
            jax.ShapeDtypeStruct((NODES // 4, 1, 128), f32),
        ),
        in_specs=[any_, any_],
        out_specs=(any_, any_),
        scratch_shapes=[
            pltpu.VMEM((4, PIECE, WIDTH), bf16),
            pltpu.VMEM((NODES // 4, 1, 128), f32),
            dma((5,)),
            dma((5,)),
        ],
        compiler_params=pltpu.CompilerParams(vmem_limit_bytes=60 * 2**20),
        name="put",
    )(cents, lse)
    return cents.reshape(KIDS, WIDTH), lse.reshape(NODES * CAP)


def solution(mesh):
    placed = (
        P(("row", "node"), None),
        P(("row", "node")),
        P(("row", "node"), None),
        P("node"),
        P("node", None),
    )
    return jax.shard_map(
        body,
        mesh=mesh,
        in_specs=placed,
        out_specs=(P("node", None), P(("row", "node"))),
        check_vma=False,
    )
```

```python
import jax
import jax.numpy as jnp
from jax import lax
from jax.experimental import pallas as pl
from jax.experimental.pallas import tpu as pltpu
from jax.sharding import PartitionSpec as P

MESH = pl.DeviceIdType.MESH
NY, NZ, NX = 4, 8, 4
NODES = 64
CAP = 32
WIDTH = 1024
KIDS = 512
PIECE = KIDS // 4
HALF = PIECE // 2
GROUP = 8
ROWS_G = GROUP * CAP
GROUPS = NODES // GROUP
NEAR = 3
AHEAD = 3
POS = (0, 1, 3, 2)


def place():
    x, n = lax.axis_index("row"), lax.axis_index("node")
    return x, n // 16, (n // 2) % NZ, n % 2


def device(x, y, z, c):
    return x, (y * NZ + z) * 2 + c


def offsets(k):
    g, i = k // GROUP, k % GROUP
    h = (i + 1) // 2
    v = (g + i) % 8
    return v // 2, (h + (1 - i % 2) * (NZ - 2 * h)) % NZ, v % 2


def target(k):
    x, y, z, c = place()
    d4, dz, dc = offsets(k)
    t, pz = (c + dc) % 2, (z + dz) % NZ
    px, py = (x + t * d4) % NX, (y + (1 - t) * d4) % NY
    yj = (1 - t) * py + t * px
    return device(px, py, pz, t), (yj * NZ + pz) * 2 + t


def source(k):
    x, y, z, c = place()
    d4, dz, dc = offsets(k)
    return device((x + c * (NX - d4)) % NX, (y + (1 - c) * (NY - d4)) % NY, (z + NZ - dz) % NZ, (c + dc) % 2)


def ring(d):
    x, y, z, c = place()
    return device((x + (1 - c) * d) % NX, (y + c * d) % NY, z, c)


def across(d):
    x, y, z, c = place()
    return device((x + d) % NX, y, z, c)


def along(d):
    x, y, z, c = place()
    return device(x, y, (z + d) % NZ, c)


def down(d):
    x, y, z, c = place()
    return device(x, (y + d) % NY, z, c)


def send(src, dst, ssem, rsem, to):
    return pltpu.make_async_remote_copy(
        src_ref=src, dst_ref=dst, send_sem=ssem, recv_sem=rsem, device_id=to, device_id_type=MESH
    )


def lane():
    return lax.broadcasted_iota(jnp.int32, (1, 128), 1)


def column(row):
    r = lax.broadcasted_iota(jnp.int32, (128, 128), 0)
    q = lax.broadcasted_iota(jnp.int32, (128, 128), 1)
    return jnp.sum(jnp.where(r == q, jnp.broadcast_to(row, (128, 128)), 0.0), axis=1, keepdims=True)


def row_of(col):
    r = lax.broadcasted_iota(jnp.int32, (128, 128), 0)
    q = lax.broadcasted_iota(jnp.int32, (128, 128), 1)
    return jnp.sum(jnp.where(r == q, jnp.broadcast_to(col, (128, 128)), 0.0), axis=0, keepdims=True)


def loop(n, body):
    lax.fori_loop(0, n, lambda i, carry: (body(i), carry)[1], 0)


def kernel(
    emb, rowpar_any, fill_any, kids, cent,
    out_c, out_l,
    xs, rowpar, fill, tags, tagr, tagm, kidr, kidc, cen, csq, resp, score, sums, massl, massr, massg,
    snd, relay, got, fin, lsem, lsnd, lret,
    a2s, a2r, tags_s, tags_r, cens, cenr, kisem, rss, rsr, mss, msr, ags, agr, fws, fwr, lss, lsr, stage, stage_out, lout_sem, in_sems, go,
):
    x, y, z, c = place()
    r = (1 - c) * x + c * y
    served = ((1 - c) * y + c * x) * (NZ * 2) + z * 2 + c
    quarter = served % 4
    moved = c * jnp.minimum((x - y) * (x - y), 1)
    mirror = device(y, x, z, c)

    barrier = pltpu.get_barrier_semaphore()
    for k in range(1, NODES):
        if k % GROUP < NEAR:
            pl.semaphore_signal(barrier, inc=1, device_id=source(k), device_id_type=MESH)
    for d in (1, 2, 3):
        pl.semaphore_signal(barrier, inc=1, device_id=ring(d), device_id_type=MESH)

    @pl.when(moved == 1)
    def _():
        pl.semaphore_signal(barrier, inc=1, device_id=mirror, device_id_type=MESH)

    arrive = [
        pltpu.make_async_copy(rowpar_any, rowpar, in_sems.at[0]),
        pltpu.make_async_copy(fill_any, fill, in_sems.at[1]),
    ]
    for o in arrive:
        o.start()
    for o in arrive:
        o.wait()

    for v in range(NODES // 4):
        limit = jnp.zeros((1, 128), jnp.int32)
        for q in range(4):
            limit = jnp.where(lane() // CAP == q, fill[0, 4 * v + q], limit)
        tags[v] = jnp.where(lane() % CAP < limit, rowpar[v], -1)
    sums[...] = jnp.zeros_like(sums)
    massl[...] = jnp.zeros_like(massl)

    pl.semaphore_wait(barrier, NEAR * GROUPS - 1 + 3 + moved)

    def given(d, first):
        p = (first + d) % 4
        at = pl.ds(pl.multiple_of(p * PIECE, PIECE), PIECE)
        return (cent.at[at], cen.at[0, pl.ds(POS[d] * PIECE, PIECE)]), (kids.at[p], kidr.at[POS[d]])

    def to_mirror():
        return [
            send(src, dst, cens.at[i], sem, mirror)
            for d in range(4)
            for i, ((src, dst), sem) in enumerate(zip(given(d, x), (cenr, kisem)))
        ]

    @pl.when(moved == 1)
    def _():
        for o in to_mirror():
            o.start()

    @pl.when(moved == 0)
    def _():
        for d in range(4):
            for (src, dst), sem in zip(given(d, r), (cenr, kisem)):
                pltpu.make_async_copy(src, dst, sem).start()

    def slot_copy(k):
        to, j = target(k)
        return send(emb.at[j], xs.at[k], a2s, a2r.at[k], to)

    def slot_tags(k):
        to, j = target(k)
        return send(tags.at[j // 4], tagr.at[k], tags_s, tags_r.at[k // GROUP], to)

    def start(k):
        slot_tags(k).start()
        slot_copy(k).start()

    def start_group(g):
        loop(GROUP, lambda i: start(g * GROUP + GROUP - 1 - i))

    def tell(s):
        for d in (1, NZ - 1):
            pl.semaphore_signal(stage.at[s], inc=1, device_id=along(d), device_id_type=MESH)

    tell(0)
    loop(NEAR - 1, lambda j: start(j + 1))
    loop(NEAR * (AHEAD - 1), lambda j: start((1 + j // NEAR) * GROUP + j % NEAR))
    own = pltpu.make_async_copy(emb.at[served], xs.at[0], a2r.at[0])
    own.start()
    own_tags = pltpu.make_async_copy(tags.at[served // 4], tagr.at[0], tags_r.at[0])
    own_tags.start()
    pl.semaphore_wait(stage.at[0], 2)
    tell(1)
    pl.semaphore_wait(stage.at[1], 2)
    tell(2)
    pl.semaphore_wait(stage.at[2], 2)
    n = GROUP - NEAR
    loop(AHEAD * n, lambda j: start((j // n) * GROUP + GROUP - 1 - j % n))

    pltpu.make_async_copy(kids, kidr, kisem).wait()
    for p in range(4):
        kidc[p * PIECE:(p + 1) * PIECE, :] = column(kidr[p].astype(jnp.float32))
    pltpu.make_async_copy(cent, cen.at[0], cenr).wait()

    def norms(it, at):
        csq[at, :] = (0.5 * WIDTH**-0.5) * jnp.sum(
            jnp.square(cen[it, at, :].astype(jnp.float32)), axis=1, keepdims=True
        )

    loop(4, lambda p: norms(0, pl.ds(pl.multiple_of(p * PIECE, PIECE), PIECE)))

    def merge(v):
        total = jnp.zeros((1, 128), jnp.int32)
        for q in range(4):
            turned = pltpu.roll(tagr[4 * v + q], ((q + 4 - quarter) % 4) * CAP, 1)
            total = jnp.where(lane() // CAP == q, turned, total)
        tagm[v] = total.astype(jnp.float32)

    def rows_of(g):
        return xs[pl.ds(g * GROUP, GROUP)].reshape(ROWS_G, WIDTH)

    def products(children, rows):
        return lax.dot_general(children, rows, (((1,), (1,)), ((), ())), preferred_element_type=jnp.float32)

    def soften(g, dots):
        tag = jnp.concatenate([tagm[2 * g], tagm[2 * g + 1]], axis=1)
        score = dots * (WIDTH**-0.5) - csq[...]
        score = jnp.where(kidc[...] == tag, score, -1e30)
        top = jnp.max(score, axis=0, keepdims=True)
        expo = jnp.exp(score - top)
        total = jnp.sum(expo, axis=0, keepdims=True)
        live = tag >= 0.0
        weight = (expo * jnp.where(live, 1.0 / total, 0.0)).astype(jnp.bfloat16)
        return weight, jnp.where(live, top + jnp.log(total), 0.0)

    def add_mass(weight):
        wide = weight.astype(jnp.float32)
        massl[...] += wide[:, :128] + wide[:, 128:]

    def group_one(g):
        def arrived(i):
            pltpu.make_async_copy(emb.at[0], xs.at[g * GROUP + i], a2r.at[g * GROUP + i]).wait()

        loop(GROUP, arrived)

        @pl.when(g + AHEAD < GROUPS)
        def _():
            start_group(g + AHEAD)

        group_tags = tagr.at[pl.ds(g * GROUP, GROUP)]
        pltpu.make_async_copy(group_tags, group_tags, tags_r.at[g]).wait()
        merge(2 * g)
        merge(2 * g + 1)
        rows = rows_of(g)
        weight, _ = soften(g, products(cen[0], rows))
        sums[...] += jnp.dot(weight, rows, preferred_element_type=jnp.float32)
        add_mass(weight)

    loop(GROUPS, group_one)

    def piece(d):
        return pl.ds(POS[d % 4] * PIECE, PIECE)

    def part(d, h):
        return pl.ds(POS[d % 4] * PIECE + h * HALF, HALF)

    def half(h):
        return pl.ds(h * HALF, HALF)

    def reduce_scatter(it, before, meanwhile):
        right, left = ring(1), ring(3)
        before(2)
        snd[it, 0] = sums[piece(2), :].astype(jnp.bfloat16)
        far_a = send(snd.at[it, 0, half(0)], relay.at[it, 0], rss.at[it, 0], rsr.at[it, 0], right)
        far_b = send(snd.at[it, 0, half(1)], relay.at[it, 1], rss.at[it, 1], rsr.at[it, 1], left)
        far_a.start()
        far_b.start()
        before(1)
        snd[it, 1, half(1)] = sums[part(1, 1), :].astype(jnp.bfloat16)
        near_r = send(snd.at[it, 1, half(1)], got.at[it, 0, half(1)], rss.at[it, 2], rsr.at[it, 2], right)
        near_r.start()
        before(3)
        snd[it, 2, half(0)] = sums[part(3, 0), :].astype(jnp.bfloat16)
        near_l = send(snd.at[it, 2, half(0)], got.at[it, 1, half(0)], rss.at[it, 3], rsr.at[it, 3], left)
        near_l.start()
        for p in range(4):
            massr[it, p] = row_of(jnp.sum(massl[p * PIECE:(p + 1) * PIECE, :], axis=1, keepdims=True))
        masses = [
            send(massr.at[it, POS[d]], massg.at[it, d - 1], mss.at[it, d - 1], msr.at[it, d - 1], ring(d))
            for d in (1, 2, 3)
        ]
        for m in masses:
            m.start()
        far_a.wait_recv()
        snd[it, 1, half(0)] = (sums[part(1, 0), :] + relay[it, 0].astype(jnp.float32)).astype(jnp.bfloat16)
        on_r = send(snd.at[it, 1, half(0)], got.at[it, 0, half(0)], rss.at[it, 4], rsr.at[it, 4], right)
        on_r.start()
        far_b.wait_recv()
        snd[it, 2, half(1)] = (sums[part(3, 1), :] + relay[it, 1].astype(jnp.float32)).astype(jnp.bfloat16)
        on_l = send(snd.at[it, 2, half(1)], got.at[it, 1, half(1)], rss.at[it, 5], rsr.at[it, 5], left)
        on_l.start()
        before(0)
        meanwhile()
        for m in masses:
            m.wait_recv()
        mass = 1.0 / (column(massr[it, 0] + massg[it, 0] + massg[it, 1] + massg[it, 2]) + 1.0)
        near_r.wait_recv()
        near_l.wait_recv()
        on_r.wait_recv()
        on_l.wait_recv()
        for o in (far_a, far_b, near_r, near_l, on_r, on_l, *masses):
            o.wait_send()
        total = sums[piece(0), :] + got[it, 0].astype(jnp.float32) + got[it, 1].astype(jnp.float32)
        total = total + cen[it, piece(0), :].astype(jnp.float32)
        return (total * mass).astype(jnp.bfloat16)

    def gather(it, spot, turn, right, left, after, sent):
        copies = []
        for s, (h, to, step) in enumerate(((0, right, -1), (1, left, 1), (1, right, -1), (0, left, 1))):
            copies.append(send(spot(0, h), spot(turn * step, h), ags.at[it, s], agr.at[it, s], to))
            copies[-1].start()
        after(0)
        sent(copies)
        copies[0].wait_recv()
        on_r = send(spot(3, 0), spot(3 - turn, 0), ags.at[it, 4], agr.at[it, 4], right)
        on_r.start()
        copies[1].wait_recv()
        on_l = send(spot(1, 1), spot(1 + turn, 1), ags.at[it, 5], agr.at[it, 5], left)
        on_l.start()
        copies[2].wait_recv()
        after(3)
        copies[3].wait_recv()
        after(1)
        on_r.wait_recv()
        on_l.wait_recv()
        after(2)
        for o in (on_r, on_l):
            o.wait_send()

    def all_sent(copies):
        for o in copies:
            o.wait_send()

    nothing = lambda d: None

    cen[1, piece(0), :] = reduce_scatter(0, nothing, lambda: None)

    massl[...] = jnp.zeros_like(massl)

    def score_new(d):
        if d == 3:
            return
        at = {0: pl.ds(0, PIECE), 1: pl.ds(PIECE, 2 * PIECE), 2: pl.ds(3 * PIECE, PIECE)}[d]
        norms(1, at)

        score[at, :] = products(cen[1, at, :], xs[...].reshape(NODES * CAP, WIDTH))

    gather(0, lambda d, h: cen.at[1, part(d, h)], 1, ring(1), ring(3), score_new, all_sent)

    def group_two(g):
        weight, lse = soften(g, score[:, pl.ds(pl.multiple_of(g * ROWS_G, ROWS_G), ROWS_G)])
        resp[:, pl.ds(pl.multiple_of(g * ROWS_G, ROWS_G), ROWS_G)] = weight
        add_mass(weight)
        lsem[2 * g] = lse[:, :128]
        lsem[2 * g + 1] = lse[:, 128:]

    loop(GROUPS, group_two)

    def turn(v):
        for q in range(4):
            lsnd[4 * v + q] = pltpu.roll(lsem[v], ((quarter + 4 - q) % 4) * CAP, 1)

    def back(k):
        return send(lsnd.at[k], lret.at[served], lss, lsr, source(k))

    def maximize(d):
        if d == 3:
            return
        at, n = {0: (0, PIECE), 1: (PIECE, 2 * PIECE), 2: (3 * PIECE, PIECE)}[d]

        every = xs[...].reshape(NODES * CAP, WIDTH)
        sums[pl.ds(at, n), :] = jnp.dot(resp[pl.ds(at, n), :], every, preferred_element_type=jnp.float32)

    def turn_all():
        loop(NODES // 4, turn)
        lret[served] = lsnd[0]

    fin[c, x] = reduce_scatter(1, maximize, turn_all)

    def spot(d, h):
        return fin.at[c, (x + d) % 4, half(h)]

    def swap(w):
        return send(fin.at[1, w], fin.at[0, y], fws.at[w], fwr.at[y], device(x, w, z, c))

    lout = pltpu.make_async_copy(lsem, out_l, lout_sem)

    def pass_on(d):
        w = (x + d) % 4

        @pl.when(c * (w - y) != 0)
        def _():
            swap(w).start()

        @pl.when(c * (1 + (w - y) * (w - y)) == 1)
        def _():
            fin[0, y] = fin[1, y]

        if d == 0:
            loop(NODES - 1, lambda k: back(k + 1).start())

    def first_sent(copies):
        all_sent(copies)

        @pl.when(c == 1)
        def _():
            pl.semaphore_signal(go, inc=1, device_id=device(x, y, z, 0), device_id_type=MESH)

    @pl.when(c == 0)
    def _():
        pl.semaphore_wait(go, 1)

    gather(1, spot, 0, across(1), across(3), pass_on, first_sent)

    out = pltpu.make_async_copy(fin.at[0], out_c, stage_out)

    @pl.when(c == 0)
    def _():
        out.start()

    pltpu.make_async_copy(lret.at[pl.ds(1, NODES - 1)], lret.at[pl.ds(1, NODES - 1)], lsr).wait()
    for v in range(NODES // 4):
        total = jnp.zeros((1, 128), jnp.float32)
        for q in range(4):
            total = jnp.where(lane() // CAP == q, lret[4 * v + q], total)
        lsem[v] = total
    lout.start()

    @pl.when(c == 1)
    def _():
        for d in (1, 2, 3):
            w = (y + d) % 4
            pltpu.make_async_copy(fin.at[1, w], fin.at[0, w], fwr.at[w]).wait()
        out.start()
        for d in (1, 2, 3):
            swap((y + d) % 4).wait_send()

    pltpu.make_async_copy(lsnd.at[pl.ds(1, NODES - 1)], lsnd.at[pl.ds(1, NODES - 1)], lss).wait()
    pltpu.make_async_copy(tagr.at[pl.ds(1, NODES - 1)], tagr.at[pl.ds(1, NODES - 1)], tags_s).wait()
    pltpu.make_async_copy(emb.at[pl.ds(1, NODES - 1)], xs.at[pl.ds(1, NODES - 1)], a2s).wait()

    @pl.when(moved == 1)
    def _():
        pltpu.make_async_copy(cent, cen.at[0], cens.at[0]).wait()
        pltpu.make_async_copy(kids, kidr, cens.at[1]).wait()

    lout.wait()
    out.wait()


def put(cents, lse, out_c, out_l, held, held_l, isem, osem):
    into = [pltpu.make_async_copy(cents.at[i], held.at[i], isem.at[i]) for i in range(4)]
    into.append(pltpu.make_async_copy(lse, held_l, isem.at[4]))
    out = [pltpu.make_async_copy(held.at[i], out_c.at[i], osem.at[i]) for i in range(4)]
    out.append(pltpu.make_async_copy(held_l, out_l, osem.at[4]))
    for o in into:
        o.start()
    for i, o in zip(into, out):
        i.wait()
        o.start()
    for o in out:
        o.wait()


def body(embeddings, row_parent, block_fill, child_parent, centroids):
    any_ = pl.BlockSpec(memory_space=pl.ANY)
    bf16, f32, i32, dma = jnp.bfloat16, jnp.float32, jnp.int32, pltpu.SemaphoreType.DMA
    cents, lse = pl.pallas_call(
        kernel,
        out_shape=(
            jax.ShapeDtypeStruct((4, PIECE, WIDTH), bf16),
            jax.ShapeDtypeStruct((NODES // 4, 1, 128), f32),
        ),
        in_specs=[any_] * 5,
        out_specs=(any_, any_),
        scratch_shapes=[
            pltpu.VMEM((NODES, CAP, WIDTH), bf16),
            pltpu.VMEM((NODES // 4, 1, 128), i32),
            pltpu.SMEM((1, NODES), i32),
            pltpu.VMEM((NODES // 4, 1, 128), i32),
            pltpu.VMEM((NODES, 1, 128), i32),
            pltpu.VMEM((NODES // 4, 1, 128), f32),
            pltpu.VMEM((4, 1, 128), i32),
            pltpu.VMEM((KIDS, 1), f32),
            pltpu.VMEM((2, KIDS, WIDTH), bf16),
            pltpu.VMEM((KIDS, 1), f32),
            pltpu.VMEM((KIDS, NODES * CAP), bf16),
            pltpu.VMEM((KIDS, NODES * CAP), f32),
            pltpu.VMEM((KIDS, WIDTH), f32),
            pltpu.VMEM((KIDS, 128), f32),
            pltpu.VMEM((2, 4, 1, 128), f32),
            pltpu.VMEM((2, 3, 1, 128), f32),
            pltpu.VMEM((2, 3, PIECE, WIDTH), bf16),
            pltpu.VMEM((2, 2, HALF, WIDTH), bf16),
            pltpu.VMEM((2, 2, PIECE, WIDTH), bf16),
            pltpu.VMEM((2, 4, PIECE, WIDTH), bf16),
            pltpu.VMEM((NODES // 4, 1, 128), f32),
            pltpu.VMEM((NODES, 1, 128), f32),
            pltpu.VMEM((NODES, 1, 128), f32),
            dma, dma((NODES,)), dma, dma((GROUPS,)), dma((2,)), dma, dma,
            dma((2, 6)), dma((2, 6)), dma((2, 3)), dma((2, 3)), dma((2, 6)), dma((2, 6)),
            dma((4,)), dma((4,)), dma, dma, pltpu.SemaphoreType.REGULAR((3,)), dma, dma, dma((2,)), pltpu.SemaphoreType.REGULAR,
        ],
        compiler_params=pltpu.CompilerParams(
            collective_id=1, has_side_effects=True, vmem_limit_bytes=60 * 2**20
        ),
        cost_estimate=pl.CostEstimate(flops=10**10, bytes_accessed=2**23, transcendentals=2**21),
        name="em",
    )(
        embeddings.reshape(NODES, CAP, WIDTH),
        row_parent.reshape(NODES // 4, 1, 128),
        block_fill,
        child_parent.reshape(4, 1, 128),
        centroids,
    )
    cents, lse = pl.pallas_call(
        put,
        out_shape=(
            jax.ShapeDtypeStruct((4, PIECE, WIDTH), bf16),
            jax.ShapeDtypeStruct((NODES // 4, 1, 128), f32),
        ),
        in_specs=[any_, any_],
        out_specs=(any_, any_),
        scratch_shapes=[
            pltpu.VMEM((4, PIECE, WIDTH), bf16),
            pltpu.VMEM((NODES // 4, 1, 128), f32),
            dma((5,)),
            dma((5,)),
        ],
        compiler_params=pltpu.CompilerParams(vmem_limit_bytes=60 * 2**20),
        name="put",
    )(cents, lse)
    return cents.reshape(KIDS, WIDTH), lse.reshape(NODES * CAP)


def solution(mesh):
    placed = (
        P(("row", "node"), None),
        P(("row", "node")),
        P(("row", "node"), None),
        P("node"),
        P("node", None),
    )
    return jax.shard_map(
        body,
        mesh=mesh,
        in_specs=placed,
        out_specs=(P("node", None), P(("row", "node"))),
        check_vma=False,
    )
```
